512 devices in a mesh: grp: 16 (over y, core), seq: 32 (over z, x).
Axes of the slice: x: 4, y: 8, z: 8, core: 2. Of those that a mesh axis runs over, the one named last changes fastest.
Arguments:
- attention_output: bfloat16 [8192, 8192], P('grp', 'seq'), may hold values from -6 to 6
- output_gradient: bfloat16 [8192, 8192], P('grp', 'seq'), may hold values from -6 to 6
- output_projection_weight: bfloat16 [8192, 8192], P('seq', 'grp'), may hold values from -0.0625 to 0.0625
- tenant_down_factors: bfloat16 [32, 64, 8192], P(None, None, 'seq'), may hold values from -0.0625 to 0.0625
- tenant_up_factors: bfloat16 [32, 64, 8192], P(None, None, 'seq'), may hold values from -0.0625 to 0.0625
- block_tenant_index: int32 [64], replicated, may hold values from 0 to 31, as said below
- block_valid_rows: int32 [64], replicated, may hold values from 16 to 128, as said below
- tenant_output_row: int32 [32], replicated, may hold values from 0 to 31, as said below
Outputs:
- attention_gradient: bfloat16 [8192, 8192], P('grp', 'seq')
- grad_down: float32 [32, 64, 8192], P('grp', None, 'seq')
- grad_up: float32 [32, 64, 8192], P('grp', None, 'seq')
The draws below stay inside these ranges and needn't reach their ends.
Inputs may be any that keep to these rules, and one draw needn't show every extreme that they name: `block_tenant_index`: the 4 blocks of one group belong to different tenants whose groups tenant_output_row[t] // 2 differ; in every draw one group keeps a tenant of one block of every group. `block_valid_rows`: in every group one block has all 128 rows valid. `tenant_output_row`: A permutation of the tenants.
All inputs are finite; a program needn't handle non-finite values.
Results may differ from the reference program's by a relative error of at most 0.0031.
Values may be sent and summed in bfloat16 or wider, within the bound.
A program may use at most 64 MiB of HBM per device.

```python
import jax
import jax.numpy as jnp

MODEL_WIDTH = 8192
HEAD_COUNT = 64
HEAD_WIDTH = 128
ADAPTER_RANK = 64
TPG = 2
BLOCK = 128
NB = 4
PROJ_FEATURES = 8192
TENANT_COUNT = 32
NBLOCKS = 64
TOKEN_COUNT = 8192
N_GRP = 16


def permute_groups(subkey):
    return jax.random.permutation(subkey, N_GRP - 1)


def permute_blocks(subkey):
    return jax.random.permutation(subkey, NB)


def routing(key):
    place = jax.random.permutation(jax.random.fold_in(key, 11), TENANT_COUNT).astype(jnp.int32)
    inverse = jnp.argsort(place).astype(jnp.int32)
    hottest = jax.random.randint(jax.random.fold_in(key, 12), (), 0, N_GRP)
    order_keys = jax.random.split(jax.random.fold_in(key, 13), N_GRP)
    others = jax.vmap(permute_groups)(order_keys).astype(jnp.int32)
    rest = (hottest + 1 + others[:, :NB - 1]) % N_GRP
    owners = jnp.concatenate([jnp.full((N_GRP, 1), hottest, jnp.int32), rest.astype(jnp.int32)], axis=1)
    shuffle_keys = jax.random.split(jax.random.fold_in(key, 14), N_GRP)
    shuffles = jax.vmap(permute_blocks)(shuffle_keys).astype(jnp.int32)
    owners = jnp.take_along_axis(owners, shuffles, axis=1)
    slots = jax.random.randint(jax.random.fold_in(key, 15), (N_GRP, NB), 0, TPG)
    tenants = inverse[owners * TPG + slots].reshape(-1)
    return (tenants.astype(jnp.int32), place)


def draw_block_tenant_index(key, part):
    return routing(key)[0]


def draw_tenant_output_row(key, part):
    return routing(key)[1]


def draw_block_valid_rows(key, part):
    counts = jax.random.randint(jax.random.fold_in(key, 21), (N_GRP, NB), BLOCK // 8, BLOCK + 1)
    fullest = jax.random.randint(jax.random.fold_in(key, 22), (N_GRP,), 0, NB)
    counts = jnp.where(jnp.arange(NB, dtype=jnp.int32)[None, :] == fullest[:, None], BLOCK, counts)
    return counts.reshape(-1).astype(jnp.int32)


def steps_of(key, dims, shards, least, top_value):
    loudness = 1.0
    for position, parts in shards:
        steps = jax.random.uniform(jax.random.fold_in(jax.random.fold_in(key, 6), position), (parts,), jnp.float32, least / len(shards), top_value / len(shards))
        loudness = loudness * jnp.repeat(jnp.exp(steps), dims[position] // parts).reshape((-1,) + (1,) * (len(dims) - 1 - position))
    return loudness


def scatter_about(own_key, dims, scale, bound, shards=(), kind=jnp.bfloat16):
    drawn = jax.random.normal(own_key, dims, jnp.float32) * scale
    if len(shards) > 0:
        drawn = steps_of(own_key, dims, shards, -0.22, 0.18) * drawn
    return jnp.clip(drawn, min=-bound, max=bound).astype(kind)


def setup_inputs(seed: int = 0) -> dict:
    key_of = jax.random.split(jax.random.key(seed), 9)
    attention_output = scatter_about(key_of[0], (TOKEN_COUNT, PROJ_FEATURES), 1.0, 6.0, ((0, 16), (1, 32)))
    output_gradient = scatter_about(key_of[1], (TOKEN_COUNT, MODEL_WIDTH), 1.0, 6.0, ((0, 16), (1, 32)))
    output_projection_weight = scatter_about(key_of[2], (PROJ_FEATURES, MODEL_WIDTH), MODEL_WIDTH ** -0.5, 0.0625, ((0, 32), (1, 16)))
    tenant_down_factors = scatter_about(key_of[3], (TENANT_COUNT, ADAPTER_RANK, PROJ_FEATURES), (HEAD_COUNT * HEAD_WIDTH) ** -0.5, 0.0625, ((2, 32),))
    tenant_up_factors = scatter_about(key_of[4], (TENANT_COUNT, ADAPTER_RANK, MODEL_WIDTH), MODEL_WIDTH ** -0.5, 0.0625, ((2, 32),))
    block_tenant_index = draw_block_tenant_index(jax.random.fold_in(key_of[8], 71), 0)
    block_valid_rows = draw_block_valid_rows(jax.random.fold_in(key_of[8], 71), 0)
    tenant_output_row = draw_tenant_output_row(jax.random.fold_in(key_of[8], 71), 0)
    return dict(attention_output=attention_output, output_gradient=output_gradient, output_projection_weight=output_projection_weight, tenant_down_factors=tenant_down_factors, tenant_up_factors=tenant_up_factors, block_tenant_index=block_tenant_index, block_valid_rows=block_valid_rows, tenant_output_row=tenant_output_row)


adapter_scale = 2.0


def reference(attention_output, output_gradient, output_projection_weight, tenant_down_factors, tenant_up_factors, block_tenant_index, block_valid_rows, tenant_output_row):
    positions = jnp.arange(TOKEN_COUNT, dtype=jnp.int32)
    limits = block_valid_rows[positions // BLOCK]
    masked = jnp.where(((positions % BLOCK) < limits)[:, None], output_gradient, jnp.zeros((), jnp.bfloat16))
    hidden_row_blocks = attention_output.reshape(NBLOCKS, BLOCK, PROJ_FEATURES).astype(jnp.float32)
    gradient_row_blocks = masked.reshape(NBLOCKS, BLOCK, MODEL_WIDTH).astype(jnp.float32)
    adapter_down_factor = tenant_down_factors[block_tenant_index].astype(jnp.float32)
    adapter_up_factor = tenant_up_factors[block_tenant_index].astype(jnp.float32)
    down_rank_product = jnp.einsum('bkh,brh->bkr', hidden_row_blocks, adapter_down_factor).astype(jnp.bfloat16)
    rank_gradient = jnp.einsum('ejz,elz->ejl', gradient_row_blocks, adapter_up_factor).astype(jnp.bfloat16)
    frozen_input_gradient = jnp.dot(masked, output_projection_weight.T, preferred_element_type=jnp.float32)
    adapter_branch_term = jnp.einsum('wtf,wfl->wtl', rank_gradient.astype(jnp.float32), adapter_down_factor).reshape(TOKEN_COUNT, PROJ_FEATURES)
    attention_gradient = (frozen_input_gradient + adapter_scale * adapter_branch_term).astype(jnp.bfloat16)
    down_gradient_panel = adapter_scale * jnp.einsum('eit,eiz->etz', rank_gradient.astype(jnp.float32), hidden_row_blocks)
    up_gradient_panel = adapter_scale * jnp.einsum('jlx,jln->jxn', down_rank_product.astype(jnp.float32), gradient_row_blocks)
    target = tenant_output_row[block_tenant_index]
    grad_down = jnp.zeros((TENANT_COUNT, ADAPTER_RANK, PROJ_FEATURES), jnp.float32).at[target].add(down_gradient_panel.astype(jnp.float32))
    grad_up = jnp.zeros((TENANT_COUNT, ADAPTER_RANK, MODEL_WIDTH), jnp.float32).at[target].add(up_gradient_panel.astype(jnp.float32))
    return attention_gradient, grad_down, grad_up
```

```python
import jax
import jax.numpy as jnp
from jax import lax
from jax.experimental import pallas as pl
from jax.experimental.pallas import tpu as pltpu
from jax.sharding import PartitionSpec as P

MESH = pl.DeviceIdType.MESH
F32 = jnp.float32
BF16 = jnp.bfloat16
BLOCK = 128
NB = 4
NY, NZ, NX = 8, 8, 4
RANK = 64
SCALE = 2.0
WIDE = 256
HOPS = ((4, 3), (3, 4))


def wrap(value, size):
    return lax.rem(value + 2 * size, size)


def kernel(
    tenant_ref,
    valid_ref,
    place_ref,
    a_ref,
    g_ref,
    w_ref,
    down_ref,
    up_ref,
    out_ref,
    grad_down_ref,
    grad_up_ref,
    masked,
    m_all,
    w_all,
    partial,
    rank_part,
    rank_x,
    rank_mid,
    rank_z,
    rank_all,
    panels,
    y_send,
    y_recv,
    x_relay,
    x_sum,
    x_in,
    adapter,
    pre_s,
    pre_r,
    w_s,
    w_r,
    sib_s,
    sib_r,
    m_s,
    m_r,
    rx_s,
    rx_r,
    rz_s,
    rz_r,
    gz_s,
    gz_r,
    gx_s,
    gx_r,
    pan_s,
    pan_r,
    ys_s,
    ys_r,
    xs_s,
    xs_r,
    loc_s,
):
    grp, seq = lax.axis_index("grp"), lax.axis_index("seq")
    y, c = lax.div(grp, 2), lax.rem(grp, 2)
    z, x = lax.div(seq, NX), lax.rem(seq, NX)
    other = 1 - c
    sib_grp = y * 2 + other

    def at(yy, cc, zz, xx):
        return (yy * 2 + cc, zz * NX + xx)

    sibling = at(y, other, z, x)
    y_next = (at(wrap(y + 1, NY), c, z, x), at(wrap(y - 1, NY), c, z, x))
    z_next = (at(y, c, wrap(z + 1, NZ), x), at(y, c, wrap(z - 1, NZ), x))
    x_peer = [at(y, c, z, wrap(x + k, NX)) for k in range(1, NX)]
    z_peer = [at(y, c, wrap(z + k, NZ), x) for k in range(1, NZ)]

    sends = []

    def send(src, dst, ssem, rsem, device):
        copy = pltpu.make_async_remote_copy(
            src_ref=src,
            dst_ref=dst,
            send_sem=ssem,
            recv_sem=rsem,
            device_id=device,
            device_id_type=MESH,
        )
        copy.start()
        sends.append(copy)
        return copy

    barrier = pltpu.get_barrier_semaphore()
    greeted = list(x_peer) + list(z_peer) + list(y_next) + [sibling]
    greeted += [at(y, other, z, wrap(x + k, NX)) for k in range(1, NX)]
    for device in greeted:
        pl.semaphore_signal(barrier, inc=1, device_id=device, device_id_type=MESH)
    pl.semaphore_wait(barrier, len(greeted))

    to_core = lax.div(x, 2)
    pre = []
    for j in range(2):
        to_x = 2 * c + j
        is_self = jnp.logical_and(to_x == x, to_core == c)
        piece = w_ref.at[:, pl.ds(j * WIDE, WIDE)]
        spot = w_all.at[y, x]
        keep = pltpu.make_async_copy(piece, spot, pre_r.at[lax.rem(x, 2)])
        move = pltpu.make_async_remote_copy(
            src_ref=piece,
            dst_ref=spot,
            send_sem=pre_s.at[j],
            recv_sem=pre_r.at[lax.rem(x, 2)],
            device_id=at(y, to_core, z, to_x),
            device_id_type=MESH,
        )
        pre.append((is_self, move))

        @pl.when(is_self)
        def _(keep=keep):
            keep.start()

        @pl.when(jnp.logical_not(is_self))
        def _(move=move):
            move.start()

    m_copy = {}

    def m_hop(direction, half, hop):
        owner = wrap(z - hop if direction == 0 else z + hop, NZ)
        src = g_ref.at[pl.ds(half * WIDE, WIDE)] if hop == 0 else m_all.at[owner, half]
        m_copy[direction, half, hop] = send(
            src,
            m_all.at[owner, half],
            m_s.at[direction, half, hop],
            m_r.at[direction, half, hop],
            z_next[direction],
        )

    for half in range(2):
        for direction in range(2):
            m_hop(direction, half, 0)
    own = [
        pltpu.make_async_copy(
            g_ref.at[pl.ds(half * WIDE, WIDE)], m_all.at[z, half], loc_s.at[half]
        )
        for half in range(2)
    ]
    for copy in own:
        copy.start()

    tenants = [tenant_ref[grp * NB + b] for b in range(NB)]
    zeros = jnp.zeros((RANK, WIDE), BF16)
    contract_last = (((1,), (1,)), ((), ()))
    contract_first = (((0,), (0,)), ((), ()))
    row = lax.broadcasted_iota(jnp.int32, (BLOCK, WIDE), 0)
    for b in range(NB):
        rows = pl.ds(b * BLOCK, BLOCK)
        kept = jnp.where(
            row < valid_ref[grp * NB + b], g_ref[rows, :].astype(F32), 0.0
        ).astype(BF16)
        masked[rows, :] = kept
        ups = jnp.concatenate([up_ref[tenants[b]], zeros], axis=0)
        downs = jnp.concatenate([zeros, down_ref[tenants[b]]], axis=0)
        rank_part[b] = lax.dot_general(
            kept, ups, contract_last, preferred_element_type=F32
        ) + lax.dot_general(a_ref[rows, :], downs, contract_last, preferred_element_type=F32)
    rx = []
    for k in range(1, NX):
        rx.append(
            send(
                rank_part.at[wrap(x + k, NX)],
                rank_x.at[k - 1],
                rx_s.at[k - 1],
                rx_r.at[k - 1],
                x_peer[k - 1],
            )
        )
    for shard in range(NX):
        partial[shard] = jnp.zeros((2 * WIDE, WIDE), F32)
    panels[8] = jnp.zeros((RANK, 2 * WIDE), F32)

    w_copy, sib_copy = {}, {}

    def w_hop(direction, j, hop):
        owner = wrap(y - hop if direction == 0 else y + hop, NY)
        spot = w_all.at[owner, 2 * c + j]
        w_copy[direction, j, hop] = send(
            spot, spot, w_s.at[direction, j, hop], w_r.at[direction, j, hop], y_next[direction]
        )

    def to_sibling(owner, slot, j):
        spot = w_all.at[owner, 2 * c + j]
        sib_copy[slot, j] = send(spot, spot, sib_s.at[slot, j], sib_r.at[slot, j], sibling)

    for j in range(2):
        pltpu.make_async_copy(
            w_ref.at[:, pl.ds(0, WIDE)], w_all.at[y, 2 * c + j], pre_r.at[j]
        ).wait()
        for direction in range(2):
            w_hop(direction, j, 0)
        to_sibling(y, 0, j)

    def w_step(hop):
        for j in range(2):
            for direction in range(2):
                last = HOPS[j][direction]
                if hop >= last:
                    continue
                w_copy[direction, j, hop].wait_recv()
                if hop + 1 < last:
                    w_hop(direction, j, hop + 1)
                owner = wrap(y - 1 - hop if direction == 0 else y + 1 + hop, NY)
                to_sibling(owner, w_slot(direction, hop), j)

    def w_slot(direction, hop):
        return 7 if hop == 3 else 1 + 2 * hop + direction

    def m_step(hop):
        for half in range(2):
            for direction in range(2):
                last = HOPS[half][direction]
                if hop >= last:
                    continue
                m_copy[direction, half, hop].wait_recv()
                if hop + 1 < last:
                    m_hop(direction, half, hop + 1)

    for copy in rx:
        copy.wait_recv()
    summed = rank_part[x] + rank_x[0] + rank_x[1] + rank_x[2]
    rank_mid[...] = summed.reshape(NZ, BLOCK // NZ, BLOCK)
    rz = []
    for k in range(1, NZ):
        rz.append(
            send(
                rank_mid.at[wrap(z + k, NZ)],
                rank_z.at[k - 1],
                rz_s.at[k - 1],
                rz_r.at[k - 1],
                z_peer[k - 1],
            )
        )
    m_step(0)
    w_step(0)
    for copy in rz:
        copy.wait_recv()
    total = rank_mid[z]
    for k in range(NZ - 1):
        total = total + rank_z[k]
    rank_all[x, z] = total.astype(BF16)
    gz = []
    for k in range(1, NZ):
        gz.append(
            send(
                rank_all.at[x, z],
                rank_all.at[x, z],
                gz_s.at[k - 1],
                gz_r.at[k - 1],
                z_peer[k - 1],
            )
        )
    m_step(1)
    for copy in gz:
        copy.wait_recv()
    gx = []
    for k in range(1, NX):
        gx.append(
            send(
                rank_all.at[x], rank_all.at[x], gx_s.at[k - 1], gx_r.at[k - 1], x_peer[k - 1]
            )
        )
    w_step(1)
    for copy in gx:
        copy.wait_recv()

    for b in range(NB):
        rows = pl.ds(b * BLOCK, BLOCK)
        ranks = rank_all[b].reshape(BLOCK, BLOCK)
        by_a = lax.dot_general(
            ranks, a_ref[rows, :], contract_first, preferred_element_type=F32
        )
        by_g = lax.dot_general(
            ranks, masked[rows, :], contract_first, preferred_element_type=F32
        )
        panels[b, :, pl.ds(0, WIDE)] = SCALE * by_a[:RANK]
        panels[b, :, pl.ds(WIDE, WIDE)] = SCALE * by_g[RANK:]
    swap = send(
        panels.at[pl.ds(0, NB)], panels.at[pl.ds(NB, NB)], pan_s, pan_r, sibling
    )
    for b in range(NB):
        rows = pl.ds(b * BLOCK, BLOCK)
        ranks = rank_all[b].reshape(BLOCK, BLOCK)
        downs = jnp.concatenate([down_ref[tenants[b]], zeros], axis=0)
        adapter[rows, :] = SCALE * jnp.dot(ranks, downs, preferred_element_type=F32)
    m_step(2)

    my_places = [place_ref[tenants[b]] for b in range(NB)]
    sib_places = [place_ref[tenant_ref[sib_grp * NB + b]] for b in range(NB)]

    def contribution(chip, slot):
        place = 2 * (2 * chip + c) + slot
        mine = theirs = 8
        for b in range(NB):
            mine = jnp.where(my_places[b] == place, b, mine)
            theirs = jnp.where(sib_places[b] == place, NB + b, theirs)
        return panels[mine] + panels[theirs]

    y_copy = {}

    def y_hop(direction, slot, hop):
        distance = HOPS[slot][direction] - hop
        chip = wrap(y + distance if direction == 0 else y - distance, NY)
        value = contribution(chip, slot)
        if hop > 0:
            value = value + y_recv[direction, slot, hop - 1]
        y_send[direction, slot, hop] = value
        y_copy[direction, slot, hop] = send(
            y_send.at[direction, slot, hop],
            y_recv.at[direction, slot, hop],
            ys_s.at[direction, slot, hop],
            ys_r.at[direction, slot, hop],
            y_next[direction],
        )

    def y_step(hop):
        for slot in range(2):
            for direction in range(2):
                if hop + 1 < HOPS[slot][direction]:
                    y_copy[direction, slot, hop].wait_recv()
                    y_hop(direction, slot, hop + 1)

    w_step(2)
    swap.wait_recv()
    for slot in range(2):
        for direction in range(2):
            y_hop(direction, slot, 0)
    m_step(3)
    for copy in own:
        copy.wait()
    for slot in range(5):
        for j in range(2):
            sib_copy[slot, j].wait_recv()

    def multiply(chip, shard):
        partial[shard] += lax.dot_general(
            m_all[chip].reshape(2 * WIDE, WIDE),
            w_all[chip, shard],
            contract_last,
            preferred_element_type=F32,
        )

    def near(n, carry):
        multiply(wrap(y + lax.div(n, NX) - 2, NY), lax.rem(n, NX))
        return carry

    lax.fori_loop(0, 5 * NX, near, 0)
    w_step(3)
    for slot in (5, 6):
        for j in range(2):
            sib_copy[slot, j].wait_recv()

    def far(n, carry):
        multiply(wrap(y + 3 + 2 * lax.div(n, NX), NY), lax.rem(n, NX))
        return carry

    lax.fori_loop(0, 2 * NX, far, 0)
    for j in range(2):
        sib_copy[7, j].wait_recv()
    last_chip = wrap(y + 4, NY)

    x_next = (x_peer[0], x_peer[2])
    x_at = (wrap(x + 1, NX), wrap(x - 1, NX))
    opposite = wrap(x + 2, NX)
    x_copy = {}
    multiply(last_chip, opposite)
    for sub in range(2):
        for direction in range(2):
            rows = pl.ds(direction * WIDE + sub * BLOCK, BLOCK)
            x_copy[0, direction, sub] = send(
                partial.at[opposite, rows],
                x_relay.at[direction, sub],
                xs_s.at[0, direction, sub],
                xs_r.at[0, direction, sub],
                x_next[direction],
            )
    for direction in range(2):
        multiply(last_chip, x_at[direction])
        for sub in range(2):
            rows = pl.ds((1 - direction) * WIDE + sub * BLOCK, BLOCK)
            x_copy[1, direction, sub] = send(
                partial.at[x_at[direction], rows],
                x_in.at[0, direction, sub],
                xs_s.at[1, direction, sub],
                xs_r.at[1, direction, sub],
                x_next[direction],
            )
    multiply(last_chip, x)
    y_step(0)
    for sub in range(2):
        for direction in range(2):
            x_copy[0, direction, sub].wait_recv()
            rows = pl.ds(direction * WIDE + sub * BLOCK, BLOCK)
            x_sum[direction, sub] = x_relay[direction, sub] + partial[x_at[direction], rows, :]
            x_copy[2, direction, sub] = send(
                x_sum.at[direction, sub],
                x_in.at[1, direction, sub],
                xs_s.at[2, direction, sub],
                xs_r.at[2, direction, sub],
                x_next[direction],
            )
    y_step(1)
    y_step(2)
    for direction in range(2):
        for sub in range(2):
            x_copy[1, direction, sub].wait_recv()
    for sub in range(2):
        for half in range(2):
            x_copy[2, half, sub].wait_recv()
            b = half * 2 + sub
            rows = pl.ds(b * BLOCK, BLOCK)
            value = partial[x, rows, :] + x_in[1, half, sub] + x_in[0, 1 - half, sub]
            value = jnp.where(row < valid_ref[grp * NB + b], value, 0.0)
            out_ref[rows, :] = (value + adapter[rows, :]).astype(BF16)
    for slot in range(2):
        total = contribution(y, slot)
        for direction in range(2):
            last = HOPS[slot][direction] - 1
            y_copy[direction, slot, last].wait_recv()
            total = total + y_recv[direction, slot, last]
        grad_down_ref[slot] = total[:, :WIDE]
        grad_up_ref[slot] = total[:, WIDE:]
    for copy in sends:
        copy.wait_send()
    for is_self, move in pre:

        @pl.when(jnp.logical_not(is_self))
        def _(move=move):
            move.wait_send()


def solution(mesh):
    placed = (
        P("grp", "seq"),
        P("grp", "seq"),
        P("seq", "grp"),
        P(None, None, "seq"),
        P(None, None, "seq"),
        P(),
        P(),
        P(),
    )

    def step(a, g, w, down, up, tenants, valid, places):
        vmem = pl.BlockSpec(memory_space=pltpu.VMEM)
        smem = pl.BlockSpec(memory_space=pltpu.SMEM)
        dma = pltpu.SemaphoreType.DMA
        return pl.pallas_call(
            kernel,
            out_shape=(
                jax.ShapeDtypeStruct((NB * BLOCK, WIDE), BF16),
                jax.ShapeDtypeStruct((2, RANK, WIDE), F32),
                jax.ShapeDtypeStruct((2, RANK, WIDE), F32),
            ),
            in_specs=[smem] * 3 + [vmem] * 5,
            out_specs=(vmem, vmem, vmem),
            scratch_shapes=[
                pltpu.VMEM((NB * BLOCK, WIDE), BF16),
                pltpu.VMEM((NZ, 2, WIDE, WIDE), BF16),
                pltpu.VMEM((NY, NX, WIDE, WIDE), BF16),
                pltpu.VMEM((NX, NB * BLOCK, WIDE), F32),
                pltpu.VMEM((NB, BLOCK, BLOCK), F32),
                pltpu.VMEM((NX - 1, BLOCK, BLOCK), F32),
                pltpu.VMEM((NZ, BLOCK // NZ, BLOCK), F32),
                pltpu.VMEM((NZ - 1, BLOCK // NZ, BLOCK), F32),
                pltpu.VMEM((NX, NZ, BLOCK // NZ, BLOCK), BF16),
                pltpu.VMEM((9, RANK, 2 * WIDE), F32),
                pltpu.VMEM((2, 2, 4, RANK, 2 * WIDE), F32),
                pltpu.VMEM((2, 2, 4, RANK, 2 * WIDE), F32),
                pltpu.VMEM((2, 2, BLOCK, WIDE), F32),
                pltpu.VMEM((2, 2, BLOCK, WIDE), F32),
                pltpu.VMEM((2, 2, 2, BLOCK, WIDE), F32),
                pltpu.VMEM((NB * BLOCK, WIDE), F32),
                dma((2,)),
                dma((2,)),
                dma((2, 2, 4)),
                dma((2, 2, 4)),
                dma((8, 2)),
                dma((8, 2)),
                dma((2, 2, 4)),
                dma((2, 2, 4)),
                dma((NX - 1,)),
                dma((NX - 1,)),
                dma((NZ - 1,)),
                dma((NZ - 1,)),
                dma((NZ - 1,)),
                dma((NZ - 1,)),
                dma((NX - 1,)),
                dma((NX - 1,)),
                dma,
                dma,
                dma((2, 2, 4)),
                dma((2, 2, 4)),
                dma((3, 2, 2)),
                dma((3, 2, 2)),
                dma((2,)),
            ],
            compiler_params=pltpu.CompilerParams(
                collective_id=0, has_side_effects=True, vmem_limit_bytes=56 << 20
            ),
        )(tenants, valid, places, a, g, w, down, up)

    return jax.shard_map(
        step,
        mesh=mesh,
        in_specs=placed,
        out_specs=(P("grp", "seq"), P("grp", None, "seq"), P("grp", None, "seq")),
        check_vma=False,
    )
```

```python
import jax
import jax.numpy as jnp
from jax import lax
from jax.experimental import pallas as pl
from jax.experimental.pallas import tpu as pltpu
from jax.sharding import PartitionSpec as P

MESH = pl.DeviceIdType.MESH
F32 = jnp.float32
BF16 = jnp.bfloat16
BLOCK = 128
NB = 4
NY, NZ, NX = 8, 8, 4
RANK = 64
SCALE = 2.0
WIDE = 256
Y_TYPE = BF16
X_TYPE = BF16
X_SUM = F32
HOPS = ((4, 3), (3, 4))


def wrap(value, size):
    return lax.rem(value + 2 * size, size)


def kernel(
    tenant_ref,
    valid_ref,
    place_ref,
    a_hbm,
    g_hbm,
    w_hbm,
    down_hbm,
    up_hbm,
    out_ref,
    grad_down_ref,
    grad_up_ref,
    a_ref,
    g_ref,
    w_ref,
    down_ref,
    up_ref,
    masked,
    m_all,
    w_all,
    partial,
    rank_part,
    rank_x,
    rank_mid,
    rank_z,
    rank_all,
    panels,
    y_send,
    y_recv,
    x_out,
    x_relay,
    x_sum,
    x_direct,
    x_far,
    adapter,
    pre_s,
    pre_r,
    w_s,
    w_r,
    sib_s,
    sib_r,
    m_s,
    m_r,
    rx_s,
    rx_r,
    rz_s,
    rz_r,
    gz_s,
    gz_r,
    gx_s,
    gx_r,
    pan_s,
    pan_r,
    ys_s,
    ys_r,
    xs_s,
    xs_r,
    loc_s,
    load_s,
):
    grp, seq = lax.axis_index("grp"), lax.axis_index("seq")
    y, c = lax.div(grp, 2), lax.rem(grp, 2)
    z, x = lax.div(seq, NX), lax.rem(seq, NX)
    other = 1 - c
    sib_grp = y * 2 + other

    def at(yy, cc, zz, xx):
        return (yy * 2 + cc, zz * NX + xx)

    sibling = at(y, other, z, x)
    y_next = (at(wrap(y + 1, NY), c, z, x), at(wrap(y - 1, NY), c, z, x))
    z_next = (at(y, c, wrap(z + 1, NZ), x), at(y, c, wrap(z - 1, NZ), x))
    x_peer = [at(y, c, z, wrap(x + k, NX)) for k in range(1, NX)]
    z_peer = [at(y, c, wrap(z + k, NZ), x) for k in range(1, NZ)]

    sends = []

    def send(src, dst, ssem, rsem, device):
        copy = pltpu.make_async_remote_copy(
            src_ref=src,
            dst_ref=dst,
            send_sem=ssem,
            recv_sem=rsem,
            device_id=device,
            device_id_type=MESH,
        )
        copy.start()
        sends.append(copy)
        return copy

    loads = [
        pltpu.make_async_copy(src, dst, load_s.at[n])
        for n, (src, dst) in enumerate(
            (
                (g_hbm, g_ref),
                (up_hbm, up_ref),
                (a_hbm, a_ref),
                (down_hbm, down_ref),
                (w_hbm, w_ref),
            )
        )
    ]
    for copy in loads:
        copy.start()

    barrier = pltpu.get_barrier_semaphore()
    greeted = list(x_peer) + list(z_peer) + list(y_next) + [sibling]
    greeted += [at(y, other, z, wrap(x + k, NX)) for k in range(1, NX)]
    for device in greeted:
        pl.semaphore_signal(barrier, inc=1, device_id=device, device_id_type=MESH)

    tenants = [tenant_ref[grp * NB + b] for b in range(NB)]
    zeros = jnp.zeros((RANK, WIDE), BF16)
    contract_last = (((1,), (1,)), ((), ()))
    contract_first = (((0,), (0,)), ((), ()))
    row = lax.broadcasted_iota(jnp.int32, (BLOCK, WIDE), 0)
    panels[8] = jnp.zeros((RANK, 2 * WIDE), F32)
    for copy in loads:
        copy.wait()
    own = [
        pltpu.make_async_copy(
            g_ref.at[pl.ds(half * WIDE, WIDE)], m_all.at[z, half], loc_s.at[half]
        )
        for half in range(2)
    ]
    for copy in own:
        copy.start()
    for b in range(NB):
        rows = pl.ds(b * BLOCK, BLOCK)
        kept = jnp.where(
            row < valid_ref[grp * NB + b], g_ref[rows, :].astype(F32), 0.0
        ).astype(BF16)
        masked[rows, :] = kept
        ups = jnp.concatenate([up_ref[tenants[b]], zeros], axis=0)
        downs = jnp.concatenate([zeros, down_ref[tenants[b]]], axis=0)
        rank_part[b] = lax.dot_general(
            kept, ups, contract_last, preferred_element_type=F32
        ) + lax.dot_general(a_ref[rows, :], downs, contract_last, preferred_element_type=F32)
    pl.semaphore_wait(barrier, len(greeted))

    def flip_of(xx, cc):
        low = lax.rem(xx, 2)
        return jnp.where(lax.div(xx, 2) == cc, low, 1 - low)

    flip = flip_of(x, c)

    def shard_of(j):
        return 2 * c + lax.rem(j + flip, 2)

    to_core = lax.div(x, 2)
    pre = []
    for j in range(2):
        to_x = 2 * c + j
        is_self = jnp.logical_and(to_x == x, to_core == c)
        piece = w_ref.at[:, pl.ds(j * WIDE, WIDE)]
        spot = w_all.at[y, x]
        chunk = lax.rem(x + flip_of(to_x, to_core), 2)
        keep = pltpu.make_async_copy(piece, spot, pre_r.at[chunk])
        move = pltpu.make_async_remote_copy(
            src_ref=piece,
            dst_ref=spot,
            send_sem=pre_s.at[j],
            recv_sem=pre_r.at[chunk],
            device_id=at(y, to_core, z, to_x),
            device_id_type=MESH,
        )
        pre.append((is_self, move))

        @pl.when(is_self)
        def _(keep=keep):
            keep.start()

        @pl.when(jnp.logical_not(is_self))
        def _(move=move):
            move.start()

    m_copy, w_copy, sib_copy = {}, {}, {}

    def m_hop(direction, half, hop):
        owner = wrap(z - hop if direction == 0 else z + hop, NZ)
        src = g_ref.at[pl.ds(half * WIDE, WIDE)] if hop == 0 else m_all.at[owner, half]
        m_copy[direction, half, hop] = send(
            src,
            m_all.at[owner, half],
            m_s.at[direction, half, hop],
            m_r.at[direction, half, hop],
            z_next[direction],
        )

    def w_hop(direction, j, hop):
        owner = wrap(y - hop if direction == 0 else y + hop, NY)
        spot = w_all.at[owner, shard_of(j)]
        w_copy[direction, j, hop] = send(
            spot, spot, w_s.at[direction, j, hop], w_r.at[direction, j, hop], y_next[direction]
        )

    def to_sibling(owner, slot, j):
        spot = w_all.at[owner, shard_of(j)]
        sib_copy[slot, j] = send(spot, spot, sib_s.at[slot, j], sib_r.at[slot, j], sibling)

    def w_slot(direction, hop):
        return 7 if hop == 3 else 1 + 2 * hop + direction

    def step(hop):
        for j in range(2):
            for direction in range(2):
                last = HOPS[j][direction]
                if hop >= last:
                    continue
                w_copy[direction, j, hop].wait_recv()
                if hop + 1 < last:
                    w_hop(direction, j, hop + 1)
                owner = wrap(y - 1 - hop if direction == 0 else y + 1 + hop, NY)
                to_sibling(owner, w_slot(direction, hop), j)
                m_copy[direction, j, hop].wait_recv()
                if hop + 1 < last:
                    m_hop(direction, j, hop + 1)

    rx = []
    for k in range(1, NX):
        rx.append(
            send(
                rank_part.at[wrap(x + k, NX)],
                rank_x.at[k - 1],
                rx_s.at[k - 1],
                rx_r.at[k - 1],
                x_peer[k - 1],
            )
        )
    for half in range(2):
        for direction in range(2):
            m_hop(direction, half, 0)
    for j in range(2):
        pltpu.make_async_copy(
            w_ref.at[:, pl.ds(0, WIDE)], w_all.at[y, shard_of(j)], pre_r.at[j]
        ).wait()
        for direction in range(2):
            w_hop(direction, j, 0)
        to_sibling(y, 0, j)
    for shard in range(NX):
        partial[shard] = jnp.zeros((2 * WIDE, WIDE), F32)

    def multiply(chip, shard):
        partial[shard] += lax.dot_general(
            m_all[chip].reshape(2 * WIDE, WIDE),
            w_all[chip, shard],
            contract_last,
            preferred_element_type=F32,
        )

    def ring_distance(a, b, size):
        ahead = wrap(a - b, size)
        return jnp.minimum(ahead, size - ahead)

    def arrived(hop):
        if hop < 0:
            slots = (0,)
        elif hop < 3:
            slots = (1 + 2 * hop, 2 + 2 * hop)
        else:
            slots = (7,)
        for slot in slots:
            for j in range(2):
                sib_copy[slot, j].wait_recv()

    def products(farthest):
        def one(chip, carry):
            far = jnp.maximum(ring_distance(chip, y, NY), ring_distance(chip, z, NZ))

            @pl.when(far == farthest)
            def _():
                for shard in range(NX):
                    multiply(chip, shard)

            return carry

        lax.fori_loop(0, NY, one, 0)

    for copy in rx:
        copy.wait_recv()
    summed = rank_part[x] + rank_x[0] + rank_x[1] + rank_x[2]
    rank_mid[...] = summed.reshape(NZ, BLOCK // NZ, BLOCK)
    rz = []
    for k in range(1, NZ):
        rz.append(
            send(
                rank_mid.at[wrap(z + k, NZ)],
                rank_z.at[k - 1],
                rz_s.at[k - 1],
                rz_r.at[k - 1],
                z_peer[k - 1],
            )
        )
    step(0)
    for copy in own:
        copy.wait()
    arrived(-1)
    products(0)
    for copy in rz:
        copy.wait_recv()
    total = rank_mid[z]
    for k in range(NZ - 1):
        total = total + rank_z[k]
    rank_all[x, z] = total.astype(BF16)
    gz = []
    for k in range(1, NZ):
        gz.append(
            send(
                rank_all.at[x, z],
                rank_all.at[x, z],
                gz_s.at[k - 1],
                gz_r.at[k - 1],
                z_peer[k - 1],
            )
        )
    step(1)
    arrived(0)
    products(1)
    for copy in gz:
        copy.wait_recv()
    gx = []
    for k in range(1, NX):
        gx.append(
            send(
                rank_all.at[x], rank_all.at[x], gx_s.at[k - 1], gx_r.at[k - 1], x_peer[k - 1]
            )
        )
    step(2)
    arrived(1)
    products(2)
    for copy in gx:
        copy.wait_recv()

    for b in range(NB):
        rows = pl.ds(b * BLOCK, BLOCK)
        ranks = rank_all[b].reshape(BLOCK, BLOCK)
        by_a = lax.dot_general(
            ranks, a_ref[rows, :], contract_first, preferred_element_type=F32
        )
        by_g = lax.dot_general(
            ranks, masked[rows, :], contract_first, preferred_element_type=F32
        )
        panels[b, :, pl.ds(0, WIDE)] = SCALE * by_a[:RANK]
        panels[b, :, pl.ds(WIDE, WIDE)] = SCALE * by_g[RANK:]
    swap = send(
        panels.at[pl.ds(0, NB)], panels.at[pl.ds(NB, NB)], pan_s, pan_r, sibling
    )
    for b in range(NB):
        rows = pl.ds(b * BLOCK, BLOCK)
        ranks = rank_all[b].reshape(BLOCK, BLOCK)
        downs = jnp.concatenate([down_ref[tenants[b]], zeros], axis=0)
        adapter[rows, :] = SCALE * jnp.dot(ranks, downs, preferred_element_type=F32)

    my_places = [place_ref[tenants[b]] for b in range(NB)]
    sib_places = [place_ref[tenant_ref[sib_grp * NB + b]] for b in range(NB)]

    def contribution(chip, slot):
        place = 2 * (2 * chip + c) + slot
        mine = theirs = 8
        for b in range(NB):
            mine = jnp.where(my_places[b] == place, b, mine)
            theirs = jnp.where(sib_places[b] == place, NB + b, theirs)
        return panels[mine] + panels[theirs]

    y_copy = {}

    def y_hop(direction, slot, hop):
        distance = HOPS[slot][direction] - hop
        chip = wrap(y + distance if direction == 0 else y - distance, NY)
        value = contribution(chip, slot)
        if hop > 0:
            value = value + y_recv[direction, slot, hop - 1].astype(F32)
        y_send[direction, slot, hop] = value.astype(Y_TYPE)
        y_copy[direction, slot, hop] = send(
            y_send.at[direction, slot, hop],
            y_recv.at[direction, slot, hop],
            ys_s.at[direction, slot, hop],
            ys_r.at[direction, slot, hop],
            y_next[direction],
        )

    def y_step(hop):
        for slot in range(2):
            for direction in range(2):
                if hop + 1 < HOPS[slot][direction]:
                    y_copy[direction, slot, hop].wait_recv()
                    y_hop(direction, slot, hop + 1)

    swap.wait_recv()
    for slot in range(2):
        for direction in range(2):
            y_hop(direction, slot, 0)
    step(3)
    arrived(2)
    products(3)
    arrived(3)
    x_next = (x_peer[0], x_peer[2])
    x_at = (wrap(x + 1, NX), wrap(x - 1, NX))
    opposite = wrap(x + 2, NX)
    x_copy = {}

    for shard in range(NX):
        multiply(wrap(y + 4, NY), shard)

    @pl.when(y != z)
    def _():
        for shard in range(NX):
            multiply(wrap(z + 4, NZ), shard)

    def x_send(kind, direction, sub, src, dst):
        x_copy[kind, direction, sub] = send(
            src,
            dst,
            xs_s.at[kind, direction, sub],
            xs_r.at[kind, direction, sub],
            x_next[direction],
        )

    for sub in range(2):
        for direction in range(2):
            rows = pl.ds(direction * WIDE + sub * BLOCK, BLOCK)
            x_out[0, direction, sub] = partial[opposite, rows, :].astype(X_TYPE)
            x_send(0, direction, sub, x_out.at[0, direction, sub], x_relay.at[direction, sub])
    for direction in range(2):
        for sub in range(2):
            rows = pl.ds((1 - direction) * WIDE + sub * BLOCK, BLOCK)
            x_out[1, direction, sub] = partial[x_at[direction], rows, :].astype(X_TYPE)
            x_send(1, direction, sub, x_out.at[1, direction, sub], x_direct.at[direction, sub])
    y_step(0)
    for sub in range(2):
        for direction in range(2):
            x_copy[0, direction, sub].wait_recv()
            rows = pl.ds(direction * WIDE + sub * BLOCK, BLOCK)
            value = x_relay[direction, sub].astype(F32) + partial[x_at[direction], rows, :]
            x_sum[direction, sub] = value.astype(X_SUM)
            x_send(2, direction, sub, x_sum.at[direction, sub], x_far.at[direction, sub])
    y_step(1)
    y_step(2)
    for direction in range(2):
        for sub in range(2):
            x_copy[1, direction, sub].wait_recv()
    for sub in range(2):
        for half in range(2):
            x_copy[2, half, sub].wait_recv()
            b = half * 2 + sub
            rows = pl.ds(b * BLOCK, BLOCK)
            value = (
                partial[x, rows, :]
                + x_far[half, sub].astype(F32)
                + x_direct[1 - half, sub].astype(F32)
            )
            value = jnp.where(row < valid_ref[grp * NB + b], value, 0.0)
            out_ref[rows, :] = (value + adapter[rows, :]).astype(BF16)
    for slot in range(2):
        total = contribution(y, slot)
        for direction in range(2):
            last = HOPS[slot][direction] - 1
            y_copy[direction, slot, last].wait_recv()
            total = total + y_recv[direction, slot, last].astype(F32)
        grad_down_ref[slot] = total[:, :WIDE]
        grad_up_ref[slot] = total[:, WIDE:]
    for copy in sends:
        copy.wait_send()
    for is_self, move in pre:

        @pl.when(jnp.logical_not(is_self))
        def _(move=move):
            move.wait_send()


def solution(mesh):
    placed = (
        P("grp", "seq"),
        P("grp", "seq"),
        P("seq", "grp"),
        P(None, None, "seq"),
        P(None, None, "seq"),
        P(),
        P(),
        P(),
    )

    def whole(a, g, w, down, up, tenants, valid, places):
        vmem = pl.BlockSpec(memory_space=pltpu.VMEM)
        smem = pl.BlockSpec(memory_space=pltpu.SMEM)
        hbm = pl.BlockSpec(memory_space=pltpu.HBM)
        dma = pltpu.SemaphoreType.DMA
        return pl.pallas_call(
            kernel,
            out_shape=(
                pltpu.VMEM((NB * BLOCK, WIDE), BF16),
                pltpu.VMEM((2, RANK, WIDE), F32),
                pltpu.VMEM((2, RANK, WIDE), F32),
            ),
            in_specs=[smem] * 3 + [hbm] * 5,
            out_specs=(vmem, vmem, vmem),
            scratch_shapes=[
                pltpu.VMEM((NB * BLOCK, WIDE), BF16),
                pltpu.VMEM((NB * BLOCK, WIDE), BF16),
                pltpu.VMEM((WIDE, 2 * WIDE), BF16),
                pltpu.VMEM(down.shape, BF16),
                pltpu.VMEM(up.shape, BF16),
                pltpu.VMEM((NB * BLOCK, WIDE), BF16),
                pltpu.VMEM((NZ, 2, WIDE, WIDE), BF16),
                pltpu.VMEM((NY, NX, WIDE, WIDE), BF16),
                pltpu.VMEM((NX, NB * BLOCK, WIDE), F32),
                pltpu.VMEM((NB, BLOCK, BLOCK), F32),
                pltpu.VMEM((NX - 1, BLOCK, BLOCK), F32),
                pltpu.VMEM((NZ, BLOCK // NZ, BLOCK), F32),
                pltpu.VMEM((NZ - 1, BLOCK // NZ, BLOCK), F32),
                pltpu.VMEM((NX, NZ, BLOCK // NZ, BLOCK), BF16),
                pltpu.VMEM((9, RANK, 2 * WIDE), F32),
                pltpu.VMEM((2, 2, 4, RANK, 2 * WIDE), Y_TYPE),
                pltpu.VMEM((2, 2, 4, RANK, 2 * WIDE), Y_TYPE),
                pltpu.VMEM((2, 2, 2, BLOCK, WIDE), X_TYPE),
                pltpu.VMEM((2, 2, BLOCK, WIDE), X_TYPE),
                pltpu.VMEM((2, 2, BLOCK, WIDE), X_SUM),
                pltpu.VMEM((2, 2, BLOCK, WIDE), X_TYPE),
                pltpu.VMEM((2, 2, BLOCK, WIDE), X_SUM),
                pltpu.VMEM((NB * BLOCK, WIDE), F32),
                dma((2,)),
                dma((2,)),
                dma((2, 2, 4)),
                dma((2, 2, 4)),
                dma((8, 2)),
                dma((8, 2)),
                dma((2, 2, 4)),
                dma((2, 2, 4)),
                dma((NX - 1,)),
                dma((NX - 1,)),
                dma((NZ - 1,)),
                dma((NZ - 1,)),
                dma((NZ - 1,)),
                dma((NZ - 1,)),
                dma((NX - 1,)),
                dma((NX - 1,)),
                dma,
                dma,
                dma((2, 2, 4)),
                dma((2, 2, 4)),
                dma((3, 2, 2)),
                dma((3, 2, 2)),
                dma((2,)),
                dma((5,)),
            ],
            compiler_params=pltpu.CompilerParams(
                collective_id=0, has_side_effects=True, vmem_limit_bytes=56 << 20
            ),
        )(tenants, valid, places, a, g, w, down, up)

    return jax.shard_map(
        whole,
        mesh=mesh,
        in_specs=placed,
        out_specs=(P("grp", "seq"), P("grp", None, "seq"), P("grp", None, "seq")),
        check_vma=False,
    )
```

```python
import jax
import jax.numpy as jnp
from jax import lax
from jax.experimental import pallas as pl
from jax.experimental.pallas import tpu as pltpu
from jax.sharding import PartitionSpec as P

MESH = pl.DeviceIdType.MESH
F32 = jnp.float32
BF16 = jnp.bfloat16
BLOCK = 128
NB = 4
NY, NZ, NX = 8, 8, 4
RANK = 64
SCALE = 2.0
WIDE = 256
Y_TYPE = BF16
X_TYPE = BF16
X_SUM = BF16
HOPS = ((4, 3), (3, 4))


def wrap(value, size):
    return lax.rem(value + 2 * size, size)


def kernel(
    tenant_ref,
    valid_ref,
    place_ref,
    a_hbm,
    g_hbm,
    w_hbm,
    down_hbm,
    up_hbm,
    out_ref,
    grad_down_ref,
    grad_up_ref,
    a_ref,
    g_ref,
    down_ref,
    up_ref,
    masked,
    m_all,
    w_all,
    partial,
    rank_part,
    rank_x,
    rank_mid,
    rank_z,
    rank_all,
    panels,
    y_send,
    y_recv,
    x_out,
    x_relay,
    x_sum,
    x_direct,
    x_far,
    adapter,
    pre_s,
    pre_r,
    w_s,
    w_r,
    sib_s,
    sib_r,
    m_s,
    m_r,
    rx_s,
    rx_r,
    rz_s,
    rz_r,
    gz_s,
    gz_r,
    gx_s,
    gx_r,
    pan_s,
    pan_r,
    ys_s,
    ys_r,
    xs_s,
    xs_r,
    loc_s,
    load_s,
):
    grp, seq = lax.axis_index("grp"), lax.axis_index("seq")
    y, c = lax.div(grp, 2), lax.rem(grp, 2)
    z, x = lax.div(seq, NX), lax.rem(seq, NX)
    other = 1 - c
    sib_grp = y * 2 + other

    def at(yy, cc, zz, xx):
        return (yy * 2 + cc, zz * NX + xx)

    sibling = at(y, other, z, x)
    y_next = (at(wrap(y + 1, NY), c, z, x), at(wrap(y - 1, NY), c, z, x))
    z_next = (at(y, c, wrap(z + 1, NZ), x), at(y, c, wrap(z - 1, NZ), x))
    x_peer = [at(y, c, z, wrap(x + k, NX)) for k in range(1, NX)]
    z_peer = [at(y, c, wrap(z + k, NZ), x) for k in range(1, NZ)]

    sends = []

    def send(src, dst, ssem, rsem, device):
        copy = pltpu.make_async_remote_copy(
            src_ref=src,
            dst_ref=dst,
            send_sem=ssem,
            recv_sem=rsem,
            device_id=device,
            device_id_type=MESH,
        )
        copy.start()
        sends.append(copy)
        return copy

    loads = [
        pltpu.make_async_copy(src, dst, load_s.at[n])
        for n, (src, dst) in enumerate(
            (
                (g_hbm, g_ref),
                (up_hbm, up_ref),
                (a_hbm, a_ref),
                (down_hbm, down_ref),
            )
        )
    ]
    for copy in loads:
        copy.start()

    barrier = pltpu.get_barrier_semaphore()
    greeted = list(x_peer) + list(z_peer) + list(y_next) + [sibling]
    greeted += [at(y, other, z, wrap(x + k, NX)) for k in range(1, NX)]
    for device in greeted:
        pl.semaphore_signal(barrier, inc=1, device_id=device, device_id_type=MESH)

    pl.semaphore_wait(barrier, len(greeted))

    def flip_of(xx, cc):
        low = lax.rem(xx, 2)
        return jnp.where(lax.div(xx, 2) == cc, low, 1 - low)

    flip = flip_of(x, c)

    def shard_of(j):
        return 2 * c + lax.rem(j + flip, 2)

    to_core = lax.div(x, 2)
    pre = []
    for j in range(2):
        to_x = 2 * c + j
        is_self = jnp.logical_and(to_x == x, to_core == c)
        piece = w_hbm.at[:, pl.ds(j * WIDE, WIDE)]
        spot = w_all.at[y, x]
        chunk = lax.rem(x + flip_of(to_x, to_core), 2)
        keep = pltpu.make_async_copy(piece, spot, pre_r.at[chunk])
        move = pltpu.make_async_remote_copy(
            src_ref=piece,
            dst_ref=spot,
            send_sem=pre_s.at[j],
            recv_sem=pre_r.at[chunk],
            device_id=at(y, to_core, z, to_x),
            device_id_type=MESH,
        )
        pre.append((is_self, move))

        @pl.when(is_self)
        def _(keep=keep):
            keep.start()

        @pl.when(jnp.logical_not(is_self))
        def _(move=move):
            move.start()

    m_copy, w_copy, sib_copy = {}, {}, {}

    def m_hop(direction, half, hop):
        owner = wrap(z - hop if direction == 0 else z + hop, NZ)
        src = g_hbm.at[pl.ds(half * WIDE, WIDE)] if hop == 0 else m_all.at[owner, half]
        m_copy[direction, half, hop] = send(
            src,
            m_all.at[owner, half],
            m_s.at[direction, half, hop],
            m_r.at[direction, half, hop],
            z_next[direction],
        )

    def w_hop(direction, j, hop):
        owner = wrap(y - hop if direction == 0 else y + hop, NY)
        spot = w_all.at[owner, shard_of(j)]
        w_copy[direction, j, hop] = send(
            spot, spot, w_s.at[direction, j, hop], w_r.at[direction, j, hop], y_next[direction]
        )

    def to_sibling(owner, slot, j):
        spot = w_all.at[owner, shard_of(j)]
        sib_copy[slot, j] = send(spot, spot, sib_s.at[slot, j], sib_r.at[slot, j], sibling)

    def w_slot(direction, hop):
        return 7 if hop == 3 else 1 + 2 * hop + direction

    def step(hop, j):
        for direction in range(2):
            last = HOPS[j][direction]
            if hop >= last:
                continue
            m_copy[direction, j, hop].wait_recv()
            if hop + 1 < last:
                m_hop(direction, j, hop + 1)
        for direction in range(2):
            last = HOPS[j][direction]
            if hop >= last:
                continue
            w_copy[direction, j, hop].wait_recv()
            if hop + 1 < last:
                w_hop(direction, j, hop + 1)
            owner = wrap(y - 1 - hop if direction == 0 else y + 1 + hop, NY)
            to_sibling(owner, w_slot(direction, hop), j)

    for half in range(2):
        for direction in range(2):
            m_hop(direction, half, 0)
    tenants = [tenant_ref[grp * NB + b] for b in range(NB)]
    zeros = jnp.zeros((RANK, WIDE), BF16)
    contract_last = (((1,), (1,)), ((), ()))
    contract_first = (((0,), (0,)), ((), ()))
    row = lax.broadcasted_iota(jnp.int32, (BLOCK, WIDE), 0)
    panels[8] = jnp.zeros((RANK, 2 * WIDE), F32)
    for copy in loads:
        copy.wait()
    own = [
        pltpu.make_async_copy(
            g_ref.at[pl.ds(half * WIDE, WIDE)], m_all.at[z, half], loc_s.at[half]
        )
        for half in range(2)
    ]
    for copy in own:
        copy.start()
    for b in range(NB):
        rows = pl.ds(b * BLOCK, BLOCK)
        kept = jnp.where(
            row < valid_ref[grp * NB + b], g_ref[rows, :].astype(F32), 0.0
        ).astype(BF16)
        masked[rows, :] = kept
        ups = jnp.concatenate([up_ref[tenants[b]], zeros], axis=0)
        downs = jnp.concatenate([zeros, down_ref[tenants[b]]], axis=0)
        rank_part[b] = lax.dot_general(
            kept, ups, contract_last, preferred_element_type=F32
        ) + lax.dot_general(a_ref[rows, :], downs, contract_last, preferred_element_type=F32)
    rx = []
    for k in range(1, NX):
        rx.append(
            send(
                rank_part.at[wrap(x + k, NX)],
                rank_x.at[k - 1],
                rx_s.at[k - 1],
                rx_r.at[k - 1],
                x_peer[k - 1],
            )
        )
    for j in range(2):
        pltpu.make_async_copy(
            w_hbm.at[:, pl.ds(0, WIDE)], w_all.at[y, shard_of(j)], pre_r.at[j]
        ).wait()
        for direction in range(2):
            w_hop(direction, j, 0)
        to_sibling(y, 0, j)
    for shard in range(NX):
        partial[shard] = jnp.zeros((2 * WIDE, WIDE), F32)

    def multiply(chip, shard):
        partial[shard] += lax.dot_general(
            m_all[chip].reshape(2 * WIDE, WIDE),
            w_all[chip, shard],
            contract_last,
            preferred_element_type=F32,
        )

    def ring_distance(a, b, size):
        ahead = wrap(a - b, size)
        return jnp.minimum(ahead, size - ahead)

    def arrived(hop):
        if hop < 0:
            slots = (0,)
        elif hop < 3:
            slots = (1 + 2 * hop, 2 + 2 * hop)
        else:
            slots = (7,)
        for slot in slots:
            for j in range(2):
                sib_copy[slot, j].wait_recv()

    def products(farthest):
        def one(chip, carry):
            far = jnp.maximum(ring_distance(chip, y, NY), ring_distance(chip, z, NZ))

            @pl.when(far == farthest)
            def _():
                for shard in range(NX):
                    multiply(chip, shard)

            return carry

        lax.fori_loop(0, NY, one, 0)

    for copy in rx:
        copy.wait_recv()
    summed = rank_part[x] + rank_x[0] + rank_x[1] + rank_x[2]
    rank_mid[...] = summed.reshape(NZ, BLOCK // NZ, BLOCK)
    rz = []
    for k in range(1, NZ):
        rz.append(
            send(
                rank_mid.at[wrap(z + k, NZ)],
                rank_z.at[k - 1],
                rz_s.at[k - 1],
                rz_r.at[k - 1],
                z_peer[k - 1],
            )
        )
    step(0, 0)
    step(0, 1)
    for copy in rz:
        copy.wait_recv()
    total = rank_mid[z]
    for k in range(NZ - 1):
        total = total + rank_z[k]
    rank_all[x, z] = total.astype(BF16)
    gz = []
    for k in range(1, NZ):
        gz.append(
            send(
                rank_all.at[x, z],
                rank_all.at[x, z],
                gz_s.at[k - 1],
                gz_r.at[k - 1],
                z_peer[k - 1],
            )
        )
    for copy in own:
        copy.wait()
    arrived(-1)
    products(0)
    step(1, 0)
    for copy in gz:
        copy.wait_recv()
    gx = []
    for k in range(1, NX):
        gx.append(
            send(
                rank_all.at[x], rank_all.at[x], gx_s.at[k - 1], gx_r.at[k - 1], x_peer[k - 1]
            )
        )
    step(1, 1)
    arrived(0)
    products(1)
    for copy in gx:
        copy.wait_recv()

    for b in range(NB):
        rows = pl.ds(b * BLOCK, BLOCK)
        ranks = rank_all[b].reshape(BLOCK, BLOCK)
        by_a = lax.dot_general(
            ranks, a_ref[rows, :], contract_first, preferred_element_type=F32
        )
        by_g = lax.dot_general(
            ranks, masked[rows, :], contract_first, preferred_element_type=F32
        )
        panels[b, :, pl.ds(0, WIDE)] = SCALE * by_a[:RANK]
        panels[b, :, pl.ds(WIDE, WIDE)] = SCALE * by_g[RANK:]
    swap = send(
        panels.at[pl.ds(0, NB)], panels.at[pl.ds(NB, NB)], pan_s, pan_r, sibling
    )
    step(2, 0)

    my_places = [place_ref[tenants[b]] for b in range(NB)]
    sib_places = [place_ref[tenant_ref[sib_grp * NB + b]] for b in range(NB)]

    def contribution(chip, slot):
        place = 2 * (2 * chip + c) + slot
        mine = theirs = 8
        for b in range(NB):
            mine = jnp.where(my_places[b] == place, b, mine)
            theirs = jnp.where(sib_places[b] == place, NB + b, theirs)
        return panels[mine] + panels[theirs]

    y_copy = {}

    def y_hop(direction, slot, hop):
        distance = HOPS[slot][direction] - hop
        chip = wrap(y + distance if direction == 0 else y - distance, NY)
        value = contribution(chip, slot)
        if hop > 0:
            value = value + y_recv[direction, slot, hop - 1].astype(F32)
        y_send[direction, slot, hop] = value.astype(Y_TYPE)
        y_copy[direction, slot, hop] = send(
            y_send.at[direction, slot, hop],
            y_recv.at[direction, slot, hop],
            ys_s.at[direction, slot, hop],
            ys_r.at[direction, slot, hop],
            y_next[direction],
        )

    def y_step(hop):
        for slot in range(2):
            for direction in range(2):
                if hop + 1 < HOPS[slot][direction]:
                    y_copy[direction, slot, hop].wait_recv()
                    y_hop(direction, slot, hop + 1)

    swap.wait_recv()
    for slot in range(2):
        for direction in range(2):
            y_hop(direction, slot, 0)
    step(2, 1)
    arrived(1)
    products(2)
    y_step(0)
    step(3, 0)
    step(3, 1)
    arrived(2)
    products(3)

    @pl.when(y != z)
    def _():
        for shard in range(NX):
            multiply(wrap(z + 4, NZ), shard)

    arrived(3)
    x_next = (x_peer[0], x_peer[2])
    x_at = (wrap(x + 1, NX), wrap(x - 1, NX))
    opposite = wrap(x + 2, NX)
    x_copy = {}

    def x_send(kind, direction, sub, src, dst):
        x_copy[kind, direction, sub] = send(
            src,
            dst,
            xs_s.at[kind, direction, sub],
            xs_r.at[kind, direction, sub],
            x_next[direction],
        )

    last_chip = wrap(y + 4, NY)
    multiply(last_chip, opposite)
    for sub in range(2):
        for direction in range(2):
            rows = pl.ds(direction * WIDE + sub * BLOCK, BLOCK)
            x_out[0, direction, sub] = partial[opposite, rows, :].astype(X_TYPE)
            x_send(0, direction, sub, x_out.at[0, direction, sub], x_relay.at[direction, sub])
    y_step(1)
    for shard in (x_at[0], x_at[1], x):
        multiply(last_chip, shard)
    for direction in range(2):
        for sub in range(2):
            rows = pl.ds((1 - direction) * WIDE + sub * BLOCK, BLOCK)
            x_out[1, direction, sub] = partial[x_at[direction], rows, :].astype(X_TYPE)
            x_send(1, direction, sub, x_out.at[1, direction, sub], x_direct.at[direction, sub])
    for b in range(NB):
        rows = pl.ds(b * BLOCK, BLOCK)
        ranks = rank_all[b].reshape(BLOCK, BLOCK)
        downs = jnp.concatenate([down_ref[tenants[b]], zeros], axis=0)
        adapter[rows, :] = SCALE * jnp.dot(ranks, downs, preferred_element_type=F32)
    for sub in range(2):
        for direction in range(2):
            x_copy[0, direction, sub].wait_recv()
            rows = pl.ds(direction * WIDE + sub * BLOCK, BLOCK)
            value = x_relay[direction, sub].astype(F32) + partial[x_at[direction], rows, :]
            x_sum[direction, sub] = value.astype(X_SUM)
            x_send(2, direction, sub, x_sum.at[direction, sub], x_far.at[direction, sub])
        if sub == 0:
            y_step(2)
    for direction in range(2):
        for sub in range(2):
            x_copy[1, direction, sub].wait_recv()
    for sub in range(2):
        for half in range(2):
            x_copy[2, half, sub].wait_recv()
            b = half * 2 + sub
            rows = pl.ds(b * BLOCK, BLOCK)
            value = (
                partial[x, rows, :]
                + x_far[half, sub].astype(F32)
                + x_direct[1 - half, sub].astype(F32)
            )
            value = jnp.where(row < valid_ref[grp * NB + b], value, 0.0)
            out_ref[rows, :] = (value + adapter[rows, :]).astype(BF16)
    for slot in range(2):
        total = contribution(y, slot)
        for direction in range(2):
            last = HOPS[slot][direction] - 1
            y_copy[direction, slot, last].wait_recv()
            total = total + y_recv[direction, slot, last].astype(F32)
        grad_down_ref[slot] = total[:, :WIDE]
        grad_up_ref[slot] = total[:, WIDE:]
    for copy in sends:
        copy.wait_send()
    for is_self, move in pre:

        @pl.when(jnp.logical_not(is_self))
        def _(move=move):
            move.wait_send()


def solution(mesh):
    placed = (
        P("grp", "seq"),
        P("grp", "seq"),
        P("seq", "grp"),
        P(None, None, "seq"),
        P(None, None, "seq"),
        P(),
        P(),
        P(),
    )

    def whole(a, g, w, down, up, tenants, valid, places):
        vmem = pl.BlockSpec(memory_space=pltpu.VMEM)
        smem = pl.BlockSpec(memory_space=pltpu.SMEM)
        hbm = pl.BlockSpec(memory_space=pltpu.HBM)
        dma = pltpu.SemaphoreType.DMA
        return pl.pallas_call(
            kernel,
            out_shape=(
                pltpu.VMEM((NB * BLOCK, WIDE), BF16),
                pltpu.VMEM((2, RANK, WIDE), F32),
                pltpu.VMEM((2, RANK, WIDE), F32),
            ),
            in_specs=[smem] * 3 + [hbm] * 5,
            out_specs=(vmem, vmem, vmem),
            scratch_shapes=[
                pltpu.VMEM((NB * BLOCK, WIDE), BF16),
                pltpu.VMEM((NB * BLOCK, WIDE), BF16),
                pltpu.VMEM(down.shape, BF16),
                pltpu.VMEM(up.shape, BF16),
                pltpu.VMEM((NB * BLOCK, WIDE), BF16),
                pltpu.VMEM((NZ, 2, WIDE, WIDE), BF16),
                pltpu.VMEM((NY, NX, WIDE, WIDE), BF16),
                pltpu.VMEM((NX, NB * BLOCK, WIDE), F32),
                pltpu.VMEM((NB, BLOCK, BLOCK), F32),
                pltpu.VMEM((NX - 1, BLOCK, BLOCK), F32),
                pltpu.VMEM((NZ, BLOCK // NZ, BLOCK), F32),
                pltpu.VMEM((NZ - 1, BLOCK // NZ, BLOCK), F32),
                pltpu.VMEM((NX, NZ, BLOCK // NZ, BLOCK), BF16),
                pltpu.VMEM((9, RANK, 2 * WIDE), F32),
                pltpu.VMEM((2, 2, 4, RANK, 2 * WIDE), Y_TYPE),
                pltpu.VMEM((2, 2, 4, RANK, 2 * WIDE), Y_TYPE),
                pltpu.VMEM((2, 2, 2, BLOCK, WIDE), X_TYPE),
                pltpu.VMEM((2, 2, BLOCK, WIDE), X_TYPE),
                pltpu.VMEM((2, 2, BLOCK, WIDE), X_SUM),
                pltpu.VMEM((2, 2, BLOCK, WIDE), X_TYPE),
                pltpu.VMEM((2, 2, BLOCK, WIDE), X_SUM),
                pltpu.VMEM((NB * BLOCK, WIDE), F32),
                dma((2,)),
                dma((2,)),
                dma((2, 2, 4)),
                dma((2, 2, 4)),
                dma((8, 2)),
                dma((8, 2)),
                dma((2, 2, 4)),
                dma((2, 2, 4)),
                dma((NX - 1,)),
                dma((NX - 1,)),
                dma((NZ - 1,)),
                dma((NZ - 1,)),
                dma((NZ - 1,)),
                dma((NZ - 1,)),
                dma((NX - 1,)),
                dma((NX - 1,)),
                dma,
                dma,
                dma((2, 2, 4)),
                dma((2, 2, 4)),
                dma((3, 2, 2)),
                dma((3, 2, 2)),
                dma((2,)),
                dma((4,)),
            ],
            compiler_params=pltpu.CompilerParams(
                collective_id=0, has_side_effects=True, vmem_limit_bytes=56 << 20
            ),
        )(tenants, valid, places, a, g, w, down, up)

    return jax.shard_map(
        whole,
        mesh=mesh,
        in_specs=placed,
        out_specs=(P("grp", "seq"), P("grp", None, "seq"), P("grp", None, "seq")),
        check_vma=False,
    )
```
